32 devices in a mesh: gx: 4 (over y, x), gy: 8 (over z, core).
Axes of the slice: x: 2, y: 2, z: 4, core: 2. Of those that a mesh axis runs over, the one named last changes fastest.
Arguments:
- tokens: bfloat16 [512, 16384], P(None, ('gx', 'gy')), may hold values from -6 to 6
- gate_weight: bfloat16 [16384, 26624], P('gx', 'gy'), may hold values from -0.046875 to 0.046875
- up_weight: bfloat16 [16384, 26624], P('gx', 'gy'), may hold values from -0.046875 to 0.046875
- down_weight: bfloat16 [26624, 16384], P('gy', 'gx'), may hold values from -0.0390625 to 0.0390625
- mixing: float32 [52, 52], replicated, may hold values from -0.3 to 1.2
Outputs:
- mixed: bfloat16 [512, 16384], P(None, ('gx', 'gy'))
The draws below stay inside these ranges and needn't reach their ends.
All inputs are finite; a program needn't handle non-finite values.
Results may differ from the reference program's by a relative error of at most 0.025.
Values may be sent and summed in bfloat16 or wider, within the bound.
A program may use at most 192 MiB of HBM per device.

```python
import jax
import jax.numpy as jnp
from jax import lax

D = 16384
A_POINTS = 52
B_POINTS = 512
TOKENS = 512
FF = 26624


def draw_mixing(key, part):
    first_key, second_key = jax.random.split(jax.random.fold_in(key, 7))
    spread = jax.random.uniform(first_key, (A_POINTS, A_POINTS), jnp.float32, -0.2, 0.2)
    diagonal = jax.random.uniform(second_key, (A_POINTS,), jnp.float32, 0.8, 1.2)
    identity = jnp.eye(A_POINTS, dtype=jnp.float32)
    return spread * (1.0 - identity) + identity * diagonal[:, None]


def level_of(key, dims, shards, least, top_value):
    def one(dim, parts):
        steps = jax.random.uniform(jax.random.fold_in(jax.random.fold_in(key, 6), dim), (parts,), jnp.float32, least / len(shards), top_value / len(shards))
        return jnp.repeat(jnp.exp(steps), dims[dim] // parts).reshape((-1,) + (1,) * (len(dims) - dim - 1))

    factor_of = one(*shards[0])
    for cut in shards[1:]:
        factor_of = factor_of * one(*cut)
    return factor_of


def normal_values(stream_key, shape, scale, limit, cuts=(), kind=jnp.bfloat16):
    gain = level_of(stream_key, shape, cuts, -0.22, 0.18) if cuts else 1.0
    values = jax.random.normal(stream_key, shape, jnp.float32) * scale * gain
    return jnp.minimum(jnp.maximum(values, -limit), limit).astype(kind)


def setup_inputs(seed: int = 0) -> dict:
    splits = jax.random.split(jax.random.key(seed), 6)
    tokens = normal_values(splits[0], (TOKENS, D), 1.0, 6.0, ((1, 32),))
    gate_weight = normal_values(splits[1], (D, FF), D ** -0.5, 0.046875, ((0, 4), (1, 8)))
    up_weight = normal_values(splits[2], (D, FF), D ** -0.5, 0.046875, ((0, 4), (1, 8)))
    down_weight = normal_values(splits[3], (FF, D), FF ** -0.5, 0.0390625, ((0, 8), (1, 4)))
    mixing = draw_mixing(jax.random.fold_in(splits[5], 71), 0)
    return dict(tokens=tokens, gate_weight=gate_weight, up_weight=up_weight, down_weight=down_weight, mixing=mixing)


def parity_sign(values):
    ones_count = jnp.zeros_like(values)
    for bit_place in range(20):
        ones_count = ones_count + jnp.bitwise_and(jnp.right_shift(values, bit_place), 1)
    return (1 - 2 * jnp.bitwise_and(ones_count, 1)).astype(jnp.float32)

def sylvester(matrix_order):
    indices = jnp.arange(matrix_order, dtype=jnp.int32)
    common = jnp.bitwise_and(indices[:, None], indices[None, :])
    return parity_sign(common)

def reference(tokens, gate_weight, up_weight, down_weight, mixing):
    gate = jnp.dot(tokens, gate_weight, preferred_element_type=jnp.float32)
    up_part = jnp.dot(tokens, up_weight, preferred_element_type=jnp.float32)
    hidden = (jax.nn.silu(gate) * up_part).astype(jnp.bfloat16)
    blocks = hidden.astype(jnp.float32).reshape(TOKENS, B_POINTS, A_POINTS)
    section_one = jnp.einsum('tba,ad->tbd', blocks, mixing, precision=lax.Precision.HIGHEST)
    section_two = jnp.einsum('tbd,bc->tcd', section_one, sylvester(B_POINTS), precision=lax.Precision.HIGHEST)
    rotated = (section_two / jnp.sqrt(jnp.float32(B_POINTS))).astype(jnp.bfloat16).reshape(TOKENS, FF)
    return jnp.dot(rotated, down_weight, preferred_element_type=jnp.float32).astype(jnp.bfloat16)
```

```python
import jax
import jax.numpy as jnp
from jax import lax
from jax.sharding import PartitionSpec as P

CHUNKS = 2
EXCHANGE = "perm"
REDUCE = "perm"
GATHER = "perm"


def parity_sign(values):
    ones_count = jnp.zeros_like(values)
    for bit_place in range(20):
        ones_count = ones_count + jnp.bitwise_and(jnp.right_shift(values, bit_place), 1)
    return (1 - 2 * jnp.bitwise_and(ones_count, 1)).astype(jnp.float32)


def sylvester(matrix_order):
    indices = jnp.arange(matrix_order, dtype=jnp.int32)
    common = jnp.bitwise_and(indices[:, None], indices[None, :])
    return parity_sign(common)


def swap(blocks, axis):
    size = blocks.shape[0]
    me = lax.axis_index(axis)
    got = [lax.dynamic_index_in_dim(blocks, me, 0, keepdims=False)]
    for step in range(1, size):
        block = lax.dynamic_index_in_dim(blocks, jnp.bitwise_xor(me, step), 0, keepdims=False)
        got.append(lax.ppermute(block, axis, [(p, p ^ step) for p in range(size)]))
    return got


def by_sender(got, axis):
    me = lax.axis_index(axis)
    stacked = jnp.stack(got)
    order = jnp.bitwise_xor(jnp.arange(len(got), dtype=jnp.int32), me)
    return stacked[order]


def exchange(hidden, size):
    if EXCHANGE == "a2a":
        return lax.all_to_all(hidden, "gy", split_axis=0, concat_axis=1, tiled=True)
    rows, cols = hidden.shape
    got = by_sender(swap(hidden.reshape(size, rows // size, cols), "gy"), "gy")
    return jnp.swapaxes(got, 0, 1).reshape(rows // size, size * cols)


def exchange_back(rotated, size):
    if EXCHANGE == "a2a":
        return lax.all_to_all(rotated, "gy", split_axis=1, concat_axis=0, tiled=True)
    rows, cols = rotated.shape
    blocks = jnp.swapaxes(rotated.reshape(rows, size, cols // size), 0, 1)
    got = by_sender(swap(blocks, "gy"), "gy")
    return got.reshape(rows * size, cols // size)


def send_rows(partial_value):
    size = lax.axis_size("gx")
    rows, cols = partial_value.shape
    return swap(partial_value.reshape(size, rows // size, cols), "gx")


def total(got):
    value = got[0].astype(jnp.float32)
    for block in got[1:]:
        value = value + block.astype(jnp.float32)
    return value


def gather_rows(rotated):
    if GATHER == "ag":
        return lax.all_gather(rotated, "gx", axis=0, tiled=True)
    size = lax.axis_size("gx")
    got = [rotated] + [lax.ppermute(rotated, "gx", [(p, p ^ s) for p in range(size)]) for s in range(1, size)]
    stacked = by_sender(got, "gx")
    return stacked.reshape(size * rotated.shape[0], rotated.shape[1])


def rotate(hidden, mixing, a_points):
    rows, cols = hidden.shape
    b_points = cols // a_points
    factor = 1.0 / jnp.sqrt(jnp.float32(b_points))
    signs = sylvester(b_points).astype(jnp.bfloat16)
    blocks = hidden.reshape(rows, b_points, a_points)
    across = jnp.einsum("tba,bc->tca", blocks, signs, preferred_element_type=jnp.float32)
    within = jnp.einsum("tca,ad->tcd", across, mixing, precision=lax.Precision.HIGHEST)
    return (within * factor).astype(jnp.bfloat16).reshape(rows, cols)


def after(values, *anchors):
    return lax.optimization_barrier((values, anchors))[0]


def on_device(tokens, gate_weight, up_weight, down_weight, mixing):
    size_x, size_y = lax.axis_size("gx"), lax.axis_size("gy")
    chunks = max(1, min(CHUNKS, tokens.shape[0] // (size_x * size_y)))
    segments = [lax.all_gather(rows, "gy", axis=1, tiled=True) for rows in jnp.split(tokens, chunks, axis=0)]
    sent = []
    for segment in segments:
        gate = jnp.dot(segment, gate_weight, preferred_element_type=jnp.float32).astype(jnp.bfloat16)
        up = jnp.dot(segment, up_weight, preferred_element_type=jnp.float32).astype(jnp.bfloat16)
        sent.append((send_rows(gate), send_rows(up)))
        last = (gate, up)
    if chunks > 1:
        sent[0] = after(sent[0], *last)
    parts = []
    rotated = products = None
    for gate, up in sent:
        if rotated is not None:
            gate, up = after((gate, up), rotated)
        hidden = (jax.nn.silu(total(gate)) * total(up)).astype(jnp.bfloat16)
        mixed_in = exchange(hidden, size_y)
        if products is not None:
            mixed_in = after(mixed_in, products)
        rotated = rotate(mixed_in, mixing, mixing.shape[0])
        all_rows = gather_rows(exchange_back(rotated, size_y))
        products = jnp.dot(all_rows, down_weight, preferred_element_type=jnp.float32).astype(jnp.bfloat16)
        parts.append(lax.psum_scatter(products, "gy", scatter_dimension=1, tiled=True))
    return jnp.concatenate(parts, axis=0) if chunks > 1 else parts[0]


def solution(mesh):
    placed = (P(None, ("gx", "gy")), P("gx", "gy"), P("gx", "gy"), P("gy", "gx"), P())
    return jax.shard_map(
        on_device, mesh=mesh, in_specs=placed, out_specs=P(None, ("gx", "gy")), check_vma=False
    )
```
